32 devices in a mesh: dp: 4 (over z), expert: 8 (over y, x, core).
Axes of the slice: x: 2, y: 2, z: 4, core: 2. Of those that a mesh axis runs over, the one named last changes fastest.
Arguments:
- tokens: bfloat16 [4096, 4096], P(('dp', 'expert')), may hold values from -6 to 6
- chosen: int32 [32, 128], replicated, may hold values from 0 to 4095, as said below
- gate_levels: int32 [32, 128], replicated, may hold values from 32 to 255
- expert_gate: bfloat16 [32, 4096, 768], P(('dp', 'expert')), may hold values from -0.09375 to 0.09375
- expert_up: bfloat16 [32, 4096, 768], P(('dp', 'expert')), may hold values from -0.09375 to 0.09375
- expert_down: bfloat16 [32, 768, 4096], P(('dp', 'expert')), may hold values from -0.21875 to 0.21875
- shared_gate: bfloat16 [4096, 4096], P(('dp', 'expert')), may hold values from -0.09375 to 0.09375
- shared_up: bfloat16 [4096, 4096], P(('dp', 'expert')), may hold values from -0.09375 to 0.09375
- shared_down: bfloat16 [4096, 4096], P(('dp', 'expert')), may hold values from -0.09375 to 0.09375
Outputs:
- block_out: bfloat16 [4096, 4096], P(('dp', 'expert'))
The draws below stay inside these ranges and needn't reach their ends.
Inputs may be any that keep to these rules, and one draw needn't show every extreme that they name: `chosen`: token t lies in the rows of device t // 128 (devices numbered dp-major). Each expert's 128 indices are different; at most 8 of them lie in the rows of one device, and for every expert some device gives exactly 8.
All inputs are finite; a program needn't handle non-finite values.
Results may differ from the reference program's by a relative error of at most 0.0052.
Values may be sent and summed in bfloat16 or wider, within the bound.
A program may use at most 128 MiB of HBM per device.

```python
import jax
import jax.numpy as jnp
from jax import lax

D = 4096
FFR = 768
FFS = 4096
TOK_DEV = 128
EXPERTS = 32
TOKENS = 4096
CAP = 128
SLOT = 8


def draw_chosen(key, part):
    random_seed_heating, key_noise, key_favor, key_start, key_jitter = jax.random.split(key, 5)
    accelerator_roster = TOKENS // TOK_DEV
    spacing = TOK_DEV // SLOT
    softmax_sharpness = jax.random.randint(random_seed_heating, (accelerator_roster,), 0, 65536)
    jitter_affinity_addend = jax.random.randint(key_noise, (EXPERTS, accelerator_roster, SLOT), 0, 65536)
    preferred_experts = jax.random.randint(key_favor, (EXPERTS,), 0, accelerator_roster)
    affinity_increment = jnp.where(jnp.arange(accelerator_roster)[None, :] == preferred_experts[:, None], 131072, 0)
    dispatch_affinity_matrix = jitter_affinity_addend + softmax_sharpness[None, :, None] + affinity_increment[:, :, None]
    slot_ids = jnp.arange(accelerator_roster * SLOT, dtype=jnp.int32).reshape(1, accelerator_roster, SLOT)
    keyed = (dispatch_affinity_matrix * (accelerator_roster * SLOT) + slot_ids).reshape(EXPERTS, accelerator_roster * SLOT)
    ignored, picked = lax.top_k(keyed, CAP)
    source = picked // SLOT
    position = picked % SLOT
    starts = jax.random.randint(key_start, (EXPERTS, accelerator_roster), 0, TOK_DEV)
    jitters = jax.random.randint(key_jitter, (EXPERTS, accelerator_roster * SLOT), 0, spacing)
    start_of = jnp.take_along_axis(starts, source, axis=1)
    jitter_of = jnp.take_along_axis(jitters, picked, axis=1)
    offset = (start_of + position * spacing + jitter_of) % TOK_DEV
    return (source * TOK_DEV + offset).astype(jnp.int32)


def with_ends(array, key, smallest, largest):
    place = [jax.random.randint(jax.random.fold_in(key, axis), (), 0, length) for axis, length in enumerate(array.shape)]
    longest = array.shape.index(max(array.shape))
    neighbour = place[:longest] + [(place[longest] + 1) % array.shape[longest]] + place[longest + 1:]
    return array.at[tuple(place)].set(smallest).at[tuple(neighbour)].set(largest)


def shard_levels(own_key, extent, pieces, low, high):
    gain = 1.0
    for axis_at, blocks in pieces:
        heights = jax.random.uniform(jax.random.fold_in(jax.random.fold_in(own_key, 6), axis_at), (blocks,), jnp.float32, low / len(pieces), high / len(pieces))
        gain = gain * jnp.repeat(jnp.exp(heights), extent[axis_at] // blocks).reshape((-1,) + (1,) * (len(extent) - 1 - axis_at))
    return gain


def normal_values(rng, extent, spread, bound, pieces=(), kind=jnp.bfloat16):
    level = shard_levels(rng, extent, pieces, -0.22, 0.18) if pieces else 1.0
    drawn = jax.random.normal(rng, extent, jnp.float32) * spread * level
    return jnp.minimum(jnp.maximum(drawn, -bound), bound).astype(kind)


def setup_inputs(seed: int = 0) -> dict:
    splits = jax.random.split(jax.random.key(seed), 10)
    return {
        "tokens": normal_values(splits[0], (TOKENS, D), 1.0, 6.0, ((0, 32),)),
        "chosen": draw_chosen(jax.random.fold_in(splits[9], 71), 0),
        "gate_levels": with_ends(jax.random.randint(splits[2], (EXPERTS, CAP), 32, 256), jax.random.fold_in(splits[2], 1), 32, 255).astype(jnp.int32),
        "expert_gate": normal_values(splits[3], (EXPERTS, D, FFR), D ** -0.5, 0.09375, ((0, 32),)),
        "expert_up": normal_values(splits[4], (EXPERTS, D, FFR), D ** -0.5, 0.09375, ((0, 32),)),
        "expert_down": normal_values(splits[5], (EXPERTS, FFR, D), FFR ** -0.5, 0.21875, ((0, 32),)),
        "shared_gate": normal_values(splits[6], (FFS, D), D ** -0.5, 0.09375, ((0, 32),)),
        "shared_up": normal_values(splits[7], (FFS, D), D ** -0.5, 0.09375, ((0, 32),)),
        "shared_down": normal_values(splits[8], (FFS, D), FFS ** -0.5, 0.09375, ((0, 32),)),
    }


def expert_rows(rows, w_gate, w_up, w_down):
    gated = jnp.dot(rows, w_gate, preferred_element_type=jnp.float32)
    lifted = jnp.dot(rows, w_up, preferred_element_type=jnp.float32)
    hidden = (jax.nn.silu(gated) * lifted).astype(jnp.bfloat16)
    return jnp.dot(hidden, w_down, preferred_element_type=jnp.float32).astype(jnp.bfloat16)


def reference(tokens, chosen, gate_levels, expert_gate, expert_up, expert_down, shared_gate, shared_up, shared_down):
    def one_expert(number):
        rows = jnp.take(tokens, chosen[number], axis=0)
        return expert_rows(rows, expert_gate[number], expert_up[number], expert_down[number])

    outputs = lax.map(one_expert, jnp.arange(EXPERTS, dtype=jnp.int32))
    multiplier_factors = gate_levels.astype(jnp.float32) / 256.0
    weighted = outputs.astype(jnp.float32) * multiplier_factors[:, :, None]
    routed = jnp.zeros((TOKENS, D), jnp.float32).at[chosen.reshape(-1)].add(weighted.reshape(-1, D))

    def shared_block(rows):
        gated = jnp.dot(rows, shared_gate.T, preferred_element_type=jnp.float32)
        lifted = jnp.dot(rows, shared_up.T, preferred_element_type=jnp.float32)
        hidden = (jax.nn.silu(gated) * lifted).astype(jnp.bfloat16)
        return jnp.dot(hidden, shared_down, preferred_element_type=jnp.float32)

    shared = lax.map(shared_block, tokens.reshape(-1, TOK_DEV, D)).reshape(TOKENS, D)
    return (shared + routed).astype(jnp.bfloat16)
```

```python
import functools

import jax
import jax.numpy as jnp
from jax import lax
from jax.experimental import pallas as pl
from jax.experimental.pallas import tpu as pltpu
from jax.sharding import PartitionSpec as P

MESH = pl.DeviceIdType.MESH
TOK_CHUNKS = 4
OUT_CHUNKS = 8
SPLIT = 2
NT = (((1,), (1,)), ((), ()))


def flipped(index, mask, bits):
    out = 0
    for b in range(bits):
        bit = (index // (1 << b)) % 2
        if (mask >> b) & 1:
            bit = 1 - bit
        out = out + bit * (1 << b)
    return out


def aligned(index, size, align):
    return pl.ds(pl.multiple_of(index, align), size)


def silu_times(g, v):
    return (g / (1.0 + jnp.exp(-g)) * v).astype(jnp.bfloat16)


def slot_tables(picked, levels, d, e, n_dp, n_e, rows, slots):
    cap = picked.shape[1]
    group = n_dp * slots
    taken = n_e * group

    def spread(a):
        return jnp.concatenate([jnp.broadcast_to(a[j : j + 1], (group, cap)) for j in range(n_e)], axis=0)

    index = spread(picked)
    device = index // rows
    position = (index - device * rows).astype(jnp.float32)
    scale = spread(levels).astype(jnp.float32) / 256.0
    row_of = lax.broadcasted_iota(jnp.int32, (taken, cap), 0)
    slot = (row_of % slots).astype(jnp.float32)
    holder = (row_of // slots) % n_dp
    wanted = jnp.where(device == holder * n_e + e, 1.0, 0.0)
    below = lax.broadcasted_iota(jnp.int32, (cap, cap), 0) <= lax.broadcasted_iota(jnp.int32, (cap, cap), 1)
    rank = jnp.dot(
        wanted.astype(jnp.bfloat16), jnp.where(below, 1.0, 0.0).astype(jnp.bfloat16),
        preferred_element_type=jnp.float32,
    )
    pick = jnp.where(rank == slot + 1.0, wanted, 0.0)
    filled = jnp.sum(pick, axis=1, keepdims=True)
    place = jnp.sum(pick * position, axis=1, keepdims=True)
    weight = jnp.sum(pick * scale, axis=1, keepdims=True)
    of_slot = lax.broadcasted_iota(jnp.int32, (taken, 1), 0)
    start = ((of_slot // slots) % n_dp * rows).astype(jnp.float32)
    column = lax.broadcasted_iota(jnp.int32, (taken, n_dp * rows), 1).astype(jnp.float32)
    hit = jnp.where(column == place + start, 1.0, 0.0)
    return hit * filled, hit * weight


def block_kernel(
    n_dp, n_e, slots,
    tokens, chosen, levels, sh_gate, sh_up, sh_down, ex_gate, ex_up, ex_down,
    out,
    tok, wg, wu, wd, xg, xu, xd, sel, wsel, sbuf, rbuf, ret, hidden, xhid, rs,
    own_sem, stage_sem, tok_send, tok_recv,
    g_loc, g_dsend, g_drecv, g_ssend, g_srecv,
    w_loc, w_dsend, w_drecv, w_ssend, w_srecv,
    a_send, a_recv, r_send, r_recv, z_send, z_recv,
):
    d = lax.axis_index("dp")
    e = lax.axis_index("expert")
    rows, width = tokens.shape
    hs = sh_gate.shape[0]
    ffr = ex_gate.shape[1]
    tcol = width // TOK_CHUNKS
    col = width // OUT_CHUNKS
    bits = n_e.bit_length() - 1
    pairs = n_e // 2
    relay = pairs == 4
    group = n_dp * slots

    def dev_e(mask):
        return (d, flipped(e, mask, bits))

    barrier = pltpu.get_barrier_semaphore()
    for j in range(1, n_e):
        pl.semaphore_signal(barrier, inc=1, device_id=dev_e(j), device_id_type=MESH)
    left, right = (d - 1, e), (d + 1, e)
    has_left, has_right = d > 0, d < n_dp - 1
    for j in range(1, n_dp):
        pl.semaphore_signal(barrier, inc=1, device_id=((d + j) % n_dp, e), device_id_type=MESH)
    pl.semaphore_wait(barrier, n_e - 1 + n_dp - 1)

    def remote(src, dst, s, r, dev):
        return pltpu.make_async_remote_copy(
            src_ref=src, dst_ref=dst, send_sem=s, recv_sem=r, device_id=dev, device_id_type=MESH
        )

    near = (1, 2) if relay else tuple(range(1, pairs))

    class Unit:
        def __init__(self, src, buf, r0, rn, cols, sems, u):
            self.src, self.buf, self.r0, self.rn, self.cols = src, buf, r0, rn, cols
            self.loc, self.ds, self.dr, self.ss, self.sr = sems
            self.u = u

        def mine(self):
            return self.src.at[pl.ds(self.r0, self.rn), self.cols]

        def spot(self, mask, r0=0, rn=None):
            start = flipped(e, mask, bits) * hs + self.r0 + r0
            return self.buf.at[aligned(start, self.rn if rn is None else rn, 16), self.cols]

        def local(self):
            return pltpu.make_async_copy(self.mine(), self.spot(0), self.loc.at[self.u])

        def direct(self, k):
            return remote(self.mine(), self.spot(0), self.ds.at[self.u, k], self.dr.at[self.u, k], dev_e(2 * k))

        def direct_in(self, k):
            part = self.spot(2 * k)
            return remote(part, part, self.ds.at[self.u, k], self.dr.at[self.u, k], dev_e(2 * k))

        def onward(self, i):
            half = self.rn // 2
            part = self.spot(2 * (i + 1), i * half, half)
            return remote(part, part, self.ds.at[self.u, 3 + i], self.dr.at[self.u, 3 + i], dev_e(2 * (2 - i)))

        def onward_in(self, i):
            half = self.rn // 2
            part = self.spot(6, i * half, half)
            return remote(part, part, self.ds.at[self.u, 3 + i], self.dr.at[self.u, 3 + i], dev_e(2 * (2 - i)))

        def sibling(self, k):
            src = self.mine() if k == 0 else self.spot(2 * k)
            return remote(src, self.spot(2 * k), self.ss.at[self.u, k], self.sr.at[self.u, k], dev_e(1))

        def sibling_in(self, k):
            part = self.spot(2 * k + 1)
            return remote(part, part, self.ss.at[self.u, k], self.sr.at[self.u, k], dev_e(1))

        def begin(self):
            for k in near:
                self.direct(k).start()
            self.sibling(0).start()
            self.local().start()

        def arrive(self):
            for k in near:
                self.direct_in(k).wait_recv()
                self.sibling(k).start()

        def pass_on(self):
            if relay:
                for i in range(2):
                    self.onward(i).start()

        def spread(self):
            for k in near:
                self.direct_in(k).wait_recv()
                if relay:
                    self.onward(k - 1).start()
                self.sibling(k).start()

        def finish(self):
            if relay:
                self.onward_in(0).wait_recv()
                self.onward_in(1).wait_recv()
                self.sibling(3).start()

        def complete(self, ks):
            for k in ks:
                if k == 0:
                    self.local().wait()
                self.sibling_in(k).wait_recv()

        def drain(self):
            for k in near:
                self.direct(k).wait_send()
            if relay:
                self.onward(0).wait_send()
                self.onward(1).wait_send()
            for k in range(pairs):
                self.sibling(k).wait_send()

    g_sems = (g_loc, g_dsend, g_drecv, g_ssend, g_srecv)
    w_sems = (w_loc, w_dsend, w_drecv, w_ssend, w_srecv)
    part_rows = hs // SPLIT
    lead = [
        Unit(src, buf, p * part_rows, part_rows, pl.ds(0, width), g_sems, 2 * p + i)
        for p in range(SPLIT)
        for i, (src, buf) in enumerate(((sh_gate, wg), (sh_up, wu)))
    ]

    def out_cols(c):
        return aligned(c * col, col, col)

    def down(c):
        return Unit(sh_down, wd, 0, hs, out_cols(c), w_sems, c)

    def tok_spot(index, q):
        return tok.at[aligned(index * rows, rows, 16), pl.ds(q * tcol, tcol)]

    def tok_copy(q, h, way):
        index = d - h + 1 if way == 0 else d + h - 1
        src = tokens.at[:, pl.ds(q * tcol, tcol)] if h == 1 else tok_spot(index, q)
        return remote(
            src, tok_spot(index, q), tok_send.at[q, way, h], tok_recv.at[q, way, h], right if way == 0 else left
        )

    def tok_start(q, h):
        pl.when((d - h + 1 >= 0) & has_right)(lambda: tok_copy(q, h, 0).start())
        pl.when((d + h - 1 < n_dp) & has_left)(lambda: tok_copy(q, h, 1).start())

    def tok_wait(q, h):
        @pl.when(d - h >= 0)
        def _():
            part = tok_spot(d - h, q)
            remote(part, part, tok_send.at[q, 0, h], tok_recv.at[q, 0, h], left).wait_recv()

        @pl.when(d + h < n_dp)
        def _():
            part = tok_spot(d + h, q)
            remote(part, part, tok_send.at[q, 1, h], tok_recv.at[q, 1, h], right).wait_recv()

    def tok_drain(q, h):
        pl.when((d - h + 1 >= 0) & has_right)(lambda: tok_copy(q, h, 0).wait_send())
        pl.when((d + h - 1 < n_dp) & has_left)(lambda: tok_copy(q, h, 1).wait_send())

    def group_rows(mask):
        return aligned(flipped(e, mask, bits) * group, group, 16)

    def a_out(q, j):
        cc = pl.ds(q * tcol, tcol)
        return remote(
            sbuf.at[group_rows(j), cc], rbuf.at[group_rows(0), cc], a_send.at[q, j], a_recv.at[q, j], dev_e(j)
        )

    def a_in(q, j):
        part = rbuf.at[group_rows(j), pl.ds(q * tcol, tcol)]
        return remote(part, part, a_send.at[q, j], a_recv.at[q, j], dev_e(j))

    def a_own(q):
        cc = pl.ds(q * tcol, tcol)
        return pltpu.make_async_copy(sbuf.at[group_rows(0), cc], rbuf.at[group_rows(0), cc], a_send.at[q, 0])

    def r_out(c, j):
        cc = out_cols(c)
        return remote(
            sbuf.at[group_rows(j), cc], ret.at[group_rows(0), cc], r_send.at[c, j], r_recv.at[c, j], dev_e(j)
        )

    def r_in(c, j):
        part = ret.at[group_rows(j), out_cols(c)]
        return remote(part, part, r_send.at[c, j], r_recv.at[c, j], dev_e(j))

    def r_own(c):
        cc = out_cols(c)
        return pltpu.make_async_copy(sbuf.at[group_rows(0), cc], ret.at[group_rows(0), cc], r_send.at[c, 0])

    tok_own = pltpu.make_async_copy(tokens, tok.at[aligned(d * rows, rows, 16)], own_sem.at[0])
    tok_start(0, 1)
    for unit in lead[:2]:
        unit.begin()
    tok_start(1, 1)
    tok_own.start()
    for unit in lead[2:]:
        unit.begin()
    stage = [
        pltpu.make_async_copy(src, dst, stage_sem.at[i])
        for i, (src, dst) in enumerate(((ex_gate, xg), (ex_up, xu)))
    ]
    for copy in stage:
        copy.start()

    def fetch(c):
        return pltpu.make_async_copy(ex_down.at[:, out_cols(c)], xd.at[c % 2], stage_sem.at[2 + c % 2])

    fetch(0).start()
    fetch(1).start()

    mine = aligned(d * n_e, n_e, 8)
    with jax.named_scope("slot_tables"):
        one_hot, weighted = slot_tables(chosen[mine, :], levels[mine, :], d, e, n_dp, n_e, rows, slots)
        sel[...] = one_hot.astype(jnp.bfloat16)
        wsel[...] = weighted.T.astype(jnp.bfloat16)
    tok_own.wait()

    def dispatch(q):
        step = min(512, tcol)
        for i in range(tcol // step):
            cc = pl.ds(q * tcol + i * step, step)
            sbuf[:, cc] = jnp.dot(sel[...], tok[:, cc], preferred_element_type=jnp.float32).astype(jnp.bfloat16)
        for j in range(n_e - 1, 0, -1):
            a_out(q, j).start()
        a_own(q).start()

    def early(u):
        lead[u].arrive()
        lead[u].pass_on()

    between = {
        (0, 1): lambda: early(0),
        (0, 2): lambda: early(1),
        (1, 2): lambda: lead[2].arrive(),
        (2, 2): lambda: lead[3].arrive(),
    }
    for q in range(TOK_CHUNKS):
        for h in range(1, n_dp):
            tok_wait(q, h)
            if h < n_dp - 1:
                tok_start(q, h + 1)
            if h == 1 and q + 2 < TOK_CHUNKS:
                tok_start(q + 2, 1)
            if (q, h) in between:
                between[q, h]()
        with jax.named_scope("dispatch"):
            dispatch(q)
    lead[2].pass_on()
    lead[3].pass_on()
    down(0).begin()
    lead[0].finish()
    lead[1].finish()

    def shared_hidden(start, size):
        r = aligned(start, size, size)
        g = lax.dot_general(tok[...], wg[r, :], NT, preferred_element_type=jnp.float32)
        v = lax.dot_general(tok[...], wu[r, :], NT, preferred_element_type=jnp.float32)
        hidden[:, r] = silu_times(g, v)

    def chip_hidden(k):
        for unit in lead:
            unit.complete((k,))
        shared_hidden(flipped(e, 2 * k, bits) // 2 * (2 * hs), 2 * hs)

    if relay:
        for k in range(3):
            with jax.named_scope("hidden_near"):
                chip_hidden(k)

    for copy in stage:
        copy.wait()
    with jax.named_scope("rows_in"):
        for q in range(TOK_CHUNKS):
            for j in range(1, n_e):
                a_in(q, j).wait_recv()
            a_own(q).wait()

    @pl.loop(0, ffr // 256)
    def _(i):
        with jax.named_scope("expert_hidden"):
            f = aligned(i * 256, 256, 256)
            g = jnp.dot(rbuf[...], xg[:, f], preferred_element_type=jnp.float32)
            v = jnp.dot(rbuf[...], xu[:, f], preferred_element_type=jnp.float32)
            xhid[:, f] = silu_times(g, v)

    for q in range(TOK_CHUNKS):
        for j in range(1, n_e):
            a_out(q, j).wait_send()

    def give_back(c):
        fetch(c).wait()
        sbuf[:, out_cols(c)] = jnp.dot(
            xhid[...], xd[c % 2], preferred_element_type=jnp.float32
        ).astype(jnp.bfloat16)
        pl.when(c + 2 < OUT_CHUNKS)(lambda: fetch(c + 2).start())
        for j in range(n_e - 1, 0, -1):
            r_out(c, j).start()
        r_own(c).start()

    with jax.named_scope("give_back_0"):
        give_back(0)
    with jax.named_scope("last_weights"):
        lead[2].finish()
        lead[3].finish()
    if relay:
        with jax.named_scope("hidden_far"):
            chip_hidden(3)
    else:
        for unit in lead:
            unit.complete(range(pairs))

        @pl.loop(0, n_e * hs // 256)
        def _(i):
            shared_hidden(i * 256, 256)

    with jax.named_scope("down_0"):
        down(0).spread()
        down(1).begin()
    with jax.named_scope("give_back_1"):
        give_back(1)
    for q in range(TOK_CHUNKS):
        for h in range(1, n_dp):
            tok_drain(q, h)

    def slot_of(t, way):
        return aligned((t + 1 - way) * rows, rows, 16)

    def z_copy(c, s, way):
        t = d + s if way == 0 else d - s
        cc = out_cols(c)
        return remote(
            tok.at[aligned(t * rows, rows, 16), cc], rs.at[slot_of(t, way), cc],
            z_send.at[c, way, s], z_recv.at[c, way, s - 1], right if way == 0 else left,
        )

    def z_in(c, s, way):
        t = d + s if way == 0 else d - s
        part = rs.at[slot_of(t, way), out_cols(c)]
        return remote(part, part, z_send.at[c, way, s], z_recv.at[c, way, s], left if way == 0 else right)

    def partial(target, cc):
        r = aligned(target * rows, rows, 16)
        return jnp.dot(hidden[r, :], wd[:, cc], preferred_element_type=jnp.float32) + jnp.dot(
            wsel[r, :], ret[:, cc], preferred_element_type=jnp.float32
        )

    def hand_on(c, s, way):
        t = d + s if way == 0 else d - s
        r = aligned(t * rows, rows, 16)
        cc = out_cols(c)
        behind = has_left if way == 0 else has_right
        value = partial(t, cc)

        @pl.when(behind)
        def _():
            z_in(c, s, way).wait_recv()
            tok[r, cc] = (value + rs[slot_of(t, way), cc].astype(jnp.float32)).astype(jnp.bfloat16)

        @pl.when(jnp.logical_not(behind))
        def _():
            tok[r, cc] = value.astype(jnp.bfloat16)

        z_copy(c, s, way).start()

    def settle(c):
        cc = out_cols(c)
        value = partial(d, cc)

        @pl.when(has_left & has_right)
        def _():
            z_in(c, 0, 0).wait_recv()
            z_in(c, 0, 1).wait_recv()
            more = rs[slot_of(d, 0), cc].astype(jnp.float32) + rs[slot_of(d, 1), cc].astype(jnp.float32)
            out[:, cc] = (value + more).astype(jnp.bfloat16)

        @pl.when(jnp.logical_not(has_right))
        def _():
            z_in(c, 0, 0).wait_recv()
            out[:, cc] = (value + rs[slot_of(d, 0), cc].astype(jnp.float32)).astype(jnp.bfloat16)

        @pl.when(jnp.logical_not(has_left))
        def _():
            z_in(c, 0, 1).wait_recv()
            out[:, cc] = (value + rs[slot_of(d, 1), cc].astype(jnp.float32)).astype(jnp.bfloat16)

    def valid(c):
        return (c >= 0) & (c < OUT_CHUNKS)

    @pl.loop(0, OUT_CHUNKS + n_dp - 1)
    def _(i):
        @pl.when(i < OUT_CHUNKS)
        def _():
            unit = down(i)
            with jax.named_scope("chunk_down"):
                unit.finish()
                unit.complete(range(pairs))
            with jax.named_scope("chunk_rows"):
                for j in range(1, n_e):
                    r_in(i, j).wait_recv()
                r_own(i).wait()

        c_right, c_left = i - d, i - (n_dp - 1 - d)
        with jax.named_scope("hand_on"):
            for s in range(n_dp - 1, 0, -1):
                pl.when(valid(c_right) & (d + s < n_dp))(functools.partial(hand_on, c_right, s, 0))
                pl.when(valid(c_left) & (d - s >= 0))(functools.partial(hand_on, c_left, s, 1))

        @pl.when(i + 1 < OUT_CHUNKS)
        def _():
            with jax.named_scope("next_down"):
                down(i + 1).spread()

        @pl.when(i + 2 < OUT_CHUNKS)
        def _():
            with jax.named_scope("give_back"):
                down(i + 2).begin()
                give_back(i + 2)

        c_own = i - jnp.maximum(d, n_dp - 1 - d)
        with jax.named_scope("settle"):
            pl.when(valid(c_own))(functools.partial(settle, c_own))

    for unit in lead:
        unit.drain()

    @pl.loop(0, OUT_CHUNKS)
    def _(c):
        down(c).drain()
        for j in range(1, n_e):
            r_out(c, j).wait_send()
        for s in range(1, n_dp):
            pl.when(d + s < n_dp)(lambda: z_copy(c, s, 0).wait_send())
            pl.when(d - s >= 0)(lambda: z_copy(c, s, 1).wait_send())


def local(
    tokens, chosen, gate_levels, expert_gate, expert_up, expert_down, shared_gate, shared_up, shared_down,
    *, n_dp, n_e,
):
    rows, width = tokens.shape
    hs = shared_gate.shape[0]
    ffr = expert_gate.shape[2]
    slots = 2 * rows // (n_dp * n_e)
    taken = n_e * n_dp * slots
    pairs = n_e // 2
    links = max(pairs, 5)
    dma = pltpu.SemaphoreType.DMA
    bf16 = jnp.bfloat16
    any_spec = pl.BlockSpec(memory_space=pl.ANY)
    vmem_spec = pl.BlockSpec(memory_space=pltpu.VMEM)
    return pl.pallas_call(
        functools.partial(block_kernel, n_dp, n_e, slots),
        out_shape=jax.ShapeDtypeStruct((rows, width), bf16),
        in_specs=[any_spec] + [vmem_spec] * 2 + [any_spec] * 6,
        out_specs=vmem_spec,
        scratch_shapes=[
            pltpu.VMEM((n_dp * rows, width), bf16),
            pltpu.VMEM((n_e * hs, width), bf16),
            pltpu.VMEM((n_e * hs, width), bf16),
            pltpu.VMEM((n_e * hs, width), bf16),
            pltpu.VMEM((width, ffr), bf16),
            pltpu.VMEM((width, ffr), bf16),
            pltpu.VMEM((2, ffr, width // OUT_CHUNKS), bf16),
            pltpu.VMEM((taken, n_dp * rows), bf16),
            pltpu.VMEM((n_dp * rows, taken), bf16),
            pltpu.VMEM((taken, width), bf16),
            pltpu.VMEM((taken, width), bf16),
            pltpu.VMEM((taken, width), bf16),
            pltpu.VMEM((n_dp * rows, n_e * hs), bf16),
            pltpu.VMEM((taken, ffr), bf16),
            pltpu.VMEM(((n_dp + 1) * rows, width), bf16),
            dma((1,)),
            dma((4,)),
            dma((TOK_CHUNKS, 2, n_dp)),
            dma((TOK_CHUNKS, 2, n_dp)),
            dma((2 * SPLIT,)),
            dma((2 * SPLIT, links)),
            dma((2 * SPLIT, links)),
            dma((2 * SPLIT, pairs)),
            dma((2 * SPLIT, pairs)),
            dma((OUT_CHUNKS,)),
            dma((OUT_CHUNKS, links)),
            dma((OUT_CHUNKS, links)),
            dma((OUT_CHUNKS, pairs)),
            dma((OUT_CHUNKS, pairs)),
            dma((TOK_CHUNKS, n_e)),
            dma((TOK_CHUNKS, n_e)),
            dma((OUT_CHUNKS, n_e)),
            dma((OUT_CHUNKS, n_e)),
            dma((OUT_CHUNKS, 2, n_dp)),
            dma((OUT_CHUNKS, 2, n_dp)),
        ],
        compiler_params=pltpu.CompilerParams(
            collective_id=0, has_side_effects=True, vmem_limit_bytes=64 * 2**20 - 2**18
        ),
    )(
        tokens, chosen, gate_levels, shared_gate, shared_up, shared_down,
        expert_gate[0], expert_up[0], expert_down[0],
    )


def solution(mesh):
    both = ("dp", "expert")
    two = P(both, None)
    three = P(both, None, None)
    return jax.shard_map(
        functools.partial(local, n_dp=mesh.shape["dp"], n_e=mesh.shape["expert"]),
        mesh=mesh,
        in_specs=(two, P(), P(), three, three, three, two, two, two),
        out_specs=two,
        check_vma=False,
    )
```

```python
import functools

import jax
import jax.numpy as jnp
from jax import lax
from jax.experimental import pallas as pl
from jax.experimental.pallas import tpu as pltpu
from jax.sharding import PartitionSpec as P

MESH = pl.DeviceIdType.MESH
TOK_CHUNKS = 4
OUT_CHUNKS = 8
SPLIT = 2
NT = (((1,), (1,)), ((), ()))


def flipped(index, mask, bits):
    out = 0
    for b in range(bits):
        bit = (index // (1 << b)) % 2
        if (mask >> b) & 1:
            bit = 1 - bit
        out = out + bit * (1 << b)
    return out


def aligned(index, size, align):
    return pl.ds(pl.multiple_of(index, align), size)


def silu_times(g, v):
    return (g / (1.0 + jnp.exp(-g)) * v).astype(jnp.bfloat16)


def slot_tables(picked, levels, d, e, n_dp, n_e, rows, slots):
    cap = picked.shape[1]
    group = n_dp * slots
    taken = n_e * group

    def spread(a):
        return jnp.concatenate([jnp.broadcast_to(a[j : j + 1], (group, cap)) for j in range(n_e)], axis=0)

    index = spread(picked)
    device = index // rows
    position = (index - device * rows).astype(jnp.float32)
    scale = spread(levels).astype(jnp.float32) / 256.0
    row_of = lax.broadcasted_iota(jnp.int32, (taken, cap), 0)
    slot = (row_of % slots).astype(jnp.float32)
    holder = (row_of // slots) % n_dp
    wanted = jnp.where(device == holder * n_e + e, 1.0, 0.0)
    below = lax.broadcasted_iota(jnp.int32, (cap, cap), 0) <= lax.broadcasted_iota(jnp.int32, (cap, cap), 1)
    rank = jnp.dot(
        wanted.astype(jnp.bfloat16), jnp.where(below, 1.0, 0.0).astype(jnp.bfloat16),
        preferred_element_type=jnp.float32,
    )
    pick = jnp.where(rank == slot + 1.0, wanted, 0.0)
    filled = jnp.sum(pick, axis=1, keepdims=True)
    place = jnp.sum(pick * position, axis=1, keepdims=True)
    weight = jnp.sum(pick * scale, axis=1, keepdims=True)
    of_slot = lax.broadcasted_iota(jnp.int32, (taken, 1), 0)
    start = ((of_slot // slots) % n_dp * rows).astype(jnp.float32)
    column = lax.broadcasted_iota(jnp.int32, (taken, n_dp * rows), 1).astype(jnp.float32)
    hit = jnp.where(column == place + start, 1.0, 0.0)
    return hit * filled, hit * weight


def block_kernel(
    n_dp, n_e, slots,
    tokens, chosen, levels, sh_gate, sh_up, sh_down, ex_gate, ex_up, ex_down,
    out,
    tok, wg, wu, wd, xg, xu, xd, sel, wsel, sbuf, rbuf, ret, hidden, xhid, rs,
    own_sem, stage_sem, tok_send, tok_recv,
    g_loc, g_sent, g_direct, g_sib,
    w_loc, w_sent, w_direct, w_sib,
    a_sem, r_sem, z_send, z_recv,
):
    d = lax.axis_index("dp")
    e = lax.axis_index("expert")
    rows, width = tokens.shape
    hs = sh_gate.shape[0]
    ffr = ex_gate.shape[1]
    tcol = width // TOK_CHUNKS
    col = width // OUT_CHUNKS
    bits = n_e.bit_length() - 1
    pairs = n_e // 2
    relay = pairs == 4
    group = n_dp * slots
    taken = n_e * group

    def dev_e(mask):
        return (d, flipped(e, mask, bits))

    barrier = pltpu.get_barrier_semaphore()
    for j in range(1, n_e):
        pl.semaphore_signal(barrier, inc=1, device_id=dev_e(j), device_id_type=MESH)
    left, right = (d - 1, e), (d + 1, e)
    has_left, has_right = d > 0, d < n_dp - 1
    pl.when(has_left)(lambda: pl.semaphore_signal(barrier, inc=1, device_id=left, device_id_type=MESH))
    pl.when(has_right)(lambda: pl.semaphore_signal(barrier, inc=1, device_id=right, device_id_type=MESH))
    pl.semaphore_wait(barrier, n_e - 1 + jnp.where(has_left, 1, 0) + jnp.where(has_right, 1, 0))

    def remote(src, dst, s, r, dev):
        return pltpu.make_async_remote_copy(
            src_ref=src, dst_ref=dst, send_sem=s, recv_sem=r, device_id=dev, device_id_type=MESH
        )

    near = (1, 2) if relay else tuple(range(1, pairs))

    class Unit:
        def __init__(self, src, buf, r0, rn, cols, sems, u):
            self.src, self.buf, self.r0, self.rn, self.cols = src, buf, r0, rn, cols
            loc, sent, direct, sib = sems
            self.loc, self.sent, self.sib = loc.at[u], sent.at[u], sib.at[u]
            self.got = lambda k: direct.at[u, k]

        def mine(self):
            return self.src.at[pl.ds(self.r0, self.rn), self.cols]

        def spot(self, mask, r0=0, rn=None):
            start = flipped(e, mask, bits) * hs + self.r0 + r0
            return self.buf.at[aligned(start, self.rn if rn is None else rn, 16), self.cols]

        def blocks(self, n):
            return self.buf.at[pl.ds(0, n * self.rn), self.cols]

        def local(self):
            return pltpu.make_async_copy(self.mine(), self.spot(0), self.loc)

        def direct(self, k):
            return remote(self.mine(), self.spot(0), self.sent, self.got(k), dev_e(2 * k))

        def direct_in(self, k):
            part = self.spot(2 * k)
            return remote(part, part, self.sent, self.got(k), dev_e(2 * k))

        def onward(self, i):
            half = self.rn // 2
            part = self.spot(2 * (i + 1), i * half, half)
            return remote(part, part, self.sent, self.got(3 + i), dev_e(2 * (2 - i)))

        def onward_in(self, i):
            half = self.rn // 2
            part = self.spot(6, i * half, half)
            return remote(part, part, self.sent, self.got(3 + i), dev_e(2 * (2 - i)))

        def sibling(self, k):
            src = self.mine() if k == 0 else self.spot(2 * k)
            return remote(src, self.spot(2 * k), self.sent, self.sib, dev_e(1))

        def begin(self):
            for k in near:
                self.direct(k).start()
            self.sibling(0).start()
            self.local().start()

        def arrive(self):
            for k in near:
                self.direct_in(k).wait_recv()
                self.sibling(k).start()

        def pass_on(self):
            if relay:
                for i in range(2):
                    self.onward(i).start()

        def spread(self):
            for k in near:
                self.direct_in(k).wait_recv()
                if relay:
                    self.onward(k - 1).start()
                self.sibling(k).start()

        def finish(self):
            if relay:
                self.onward_in(0).wait_recv()
                self.onward_in(1).wait_recv()
                self.sibling(3).start()

        def complete(self):
            self.local().wait()
            part = self.blocks(pairs)
            remote(part, part, self.sent, self.sib, dev_e(1)).wait_recv()

        def drain(self):
            part = self.blocks(len(near) + (1 if relay else 0) + pairs)
            remote(part, part, self.sent, self.sib, dev_e(1)).wait_send()

    class Lead(Unit):
        def __init__(self, src, buf, r0, rn, cols, sems, u):
            loc, sent, direct, sib = sems
            self.src, self.buf, self.r0, self.rn, self.cols = src, buf, r0, rn, cols
            self.loc, self.sent = loc.at[u], sent.at[u]
            self.sib = sib.at[u, 0]
            self.got = lambda k: direct.at[u, k]
            self.sibs = lambda k: sib.at[u, k]

        def sibling(self, k):
            src = self.mine() if k == 0 else self.spot(2 * k)
            return remote(src, self.spot(2 * k), self.sent, self.sibs(k), dev_e(1))

        def complete(self, ks):
            for k in ks:
                if k == 0:
                    self.local().wait()
                part = self.spot(2 * k + 1)
                remote(part, part, self.sent, self.sibs(k), dev_e(1)).wait_recv()

    g_sems = (g_loc, g_sent, g_direct, g_sib)
    w_sems = (w_loc, w_sent, w_direct, w_sib)
    part_rows = hs // SPLIT
    lead = [
        Lead(src, buf, p * part_rows, part_rows, pl.ds(0, width), g_sems, 2 * p + i)
        for p in range(SPLIT)
        for i, (src, buf) in enumerate(((sh_gate, wg), (sh_up, wu)))
    ]

    def out_cols(c):
        return aligned(c * col, col, col)

    def down(c):
        return Unit(sh_down, wd, 0, hs, out_cols(c), w_sems, c)

    def tok_spot(index, q):
        return tok.at[aligned(index * rows, rows, 16), pl.ds(q * tcol, tcol)]

    def tok_copy(q, h, way):
        index = d - h + 1 if way == 0 else d + h - 1
        src = tokens.at[:, pl.ds(q * tcol, tcol)] if h == 1 else tok_spot(index, q)
        return remote(
            src, tok_spot(index, q), tok_send.at[q, way, h], tok_recv.at[q, way, h], right if way == 0 else left
        )

    def tok_start(q, h):
        pl.when((d - h + 1 >= 0) & has_right)(lambda: tok_copy(q, h, 0).start())
        pl.when((d + h - 1 < n_dp) & has_left)(lambda: tok_copy(q, h, 1).start())

    def tok_wait(q, h):
        @pl.when(d - h >= 0)
        def _():
            part = tok_spot(d - h, q)
            remote(part, part, tok_send.at[q, 0, h], tok_recv.at[q, 0, h], left).wait_recv()

        @pl.when(d + h < n_dp)
        def _():
            part = tok_spot(d + h, q)
            remote(part, part, tok_send.at[q, 1, h], tok_recv.at[q, 1, h], right).wait_recv()

    def tok_drain(q, h):
        pl.when((d - h + 1 >= 0) & has_right)(lambda: tok_copy(q, h, 0).wait_send())
        pl.when((d + h - 1 < n_dp) & has_left)(lambda: tok_copy(q, h, 1).wait_send())

    def group_rows(mask):
        return aligned(flipped(e, mask, bits) * group, group, 16)

    away = pl.ds(0, taken - group)

    def a_out(q, j):
        cc = pl.ds(q * tcol, tcol)
        return remote(sbuf.at[group_rows(j), cc], rbuf.at[group_rows(0), cc], a_sem.at[0, q], a_sem.at[1, q], dev_e(j))

    def a_all(q):
        part = rbuf.at[away, pl.ds(q * tcol, tcol)]
        return remote(part, part, a_sem.at[0, q], a_sem.at[1, q], dev_e(1))

    def a_own(q):
        cc = pl.ds(q * tcol, tcol)
        return pltpu.make_async_copy(sbuf.at[group_rows(0), cc], rbuf.at[group_rows(0), cc], a_sem.at[2, q])

    def r_out(c, j):
        cc = out_cols(c)
        return remote(sbuf.at[group_rows(j), cc], ret.at[group_rows(0), cc], r_sem.at[0, c], r_sem.at[1, c], dev_e(j))

    def r_all(c):
        part = ret.at[away, out_cols(c)]
        return remote(part, part, r_sem.at[0, c], r_sem.at[1, c], dev_e(1))

    def r_own(c):
        cc = out_cols(c)
        return pltpu.make_async_copy(sbuf.at[group_rows(0), cc], ret.at[group_rows(0), cc], r_sem.at[2, c])

    tok_own = pltpu.make_async_copy(tokens, tok.at[aligned(d * rows, rows, 16)], own_sem.at[0])
    tok_start(0, 1)
    for unit in lead[:2]:
        unit.begin()
    tok_start(1, 1)
    tok_own.start()
    for unit in lead[2:]:
        unit.begin()
    stage = [
        pltpu.make_async_copy(src, dst, stage_sem.at[i])
        for i, (src, dst) in enumerate(((ex_gate, xg), (ex_up, xu)))
    ]
    for copy in stage:
        copy.start()

    def fetch(c):
        return pltpu.make_async_copy(ex_down.at[:, out_cols(c)], xd.at[c % 2], stage_sem.at[2 + c % 2])

    fetch(0).start()
    fetch(1).start()

    mine = aligned(d * n_e, n_e, 8)
    one_hot, weighted = slot_tables(chosen[mine, :], levels[mine, :], d, e, n_dp, n_e, rows, slots)
    sel[...] = one_hot.astype(jnp.bfloat16)
    wsel[...] = weighted.T.astype(jnp.bfloat16)
    tok_own.wait()

    def dispatch(q):
        step = min(512, tcol)
        for i in range(tcol // step):
            cc = pl.ds(q * tcol + i * step, step)
            sbuf[:, cc] = jnp.dot(sel[...], tok[:, cc], preferred_element_type=jnp.float32).astype(jnp.bfloat16)
        for j in range(n_e - 1, 0, -1):
            a_out(q, j).start()
        a_own(q).start()

    def early(u):
        lead[u].arrive()
        lead[u].pass_on()

    between = {
        (0, 1): lambda: early(0),
        (0, 2): lambda: early(1),
        (1, 2): lambda: lead[2].arrive(),
        (2, 2): lambda: lead[3].arrive(),
    }
    for q in range(TOK_CHUNKS):
        for h in range(1, n_dp):
            tok_wait(q, h)
            if h < n_dp - 1:
                tok_start(q, h + 1)
            if h == 1 and q + 2 < TOK_CHUNKS:
                tok_start(q + 2, 1)
            if (q, h) in between:
                between[q, h]()
        dispatch(q)
    lead[2].pass_on()
    lead[3].pass_on()
    down(0).begin()
    lead[0].finish()
    lead[1].finish()

    def shared_hidden(start, size):
        r = aligned(start, size, size)
        g = lax.dot_general(tok[...], wg[r, :], NT, preferred_element_type=jnp.float32)
        v = lax.dot_general(tok[...], wu[r, :], NT, preferred_element_type=jnp.float32)
        hidden[:, r] = silu_times(g, v)

    def chip_hidden(k):
        for unit in lead:
            unit.complete((k,))
        shared_hidden(flipped(e, 2 * k, bits) // 2 * (2 * hs), 2 * hs)

    if relay:
        for k in range(3):
            chip_hidden(k)

    for copy in stage:
        copy.wait()
    for q in range(TOK_CHUNKS):
        a_all(q).wait_recv()
        a_own(q).wait()

    @pl.loop(0, ffr // 256)
    def _(i):
        f = aligned(i * 256, 256, 256)
        g = jnp.dot(rbuf[...], xg[:, f], preferred_element_type=jnp.float32)
        v = jnp.dot(rbuf[...], xu[:, f], preferred_element_type=jnp.float32)
        xhid[:, f] = silu_times(g, v)

    for q in range(TOK_CHUNKS):
        a_all(q).wait_send()

    def give_back(c):
        fetch(c).wait()
        sbuf[:, out_cols(c)] = jnp.dot(
            xhid[...], xd[c % 2], preferred_element_type=jnp.float32
        ).astype(jnp.bfloat16)
        pl.when(c + 2 < OUT_CHUNKS)(lambda: fetch(c + 2).start())
        for j in range(n_e - 1, 0, -1):
            r_out(c, j).start()
        r_own(c).start()

    give_back(0)
    lead[2].finish()
    lead[3].finish()
    if relay:
        chip_hidden(3)
    else:
        for unit in lead:
            unit.complete(range(pairs))

        @pl.loop(0, n_e * hs // 256)
        def _(i):
            shared_hidden(i * 256, 256)

    down(0).spread()
    down(1).begin()
    give_back(1)
    for q in range(TOK_CHUNKS):
        for h in range(1, n_dp):
            tok_drain(q, h)
    for unit in lead:
        unit.drain()

    def slot_of(t, way):
        return aligned((t + 1 - way) * rows, rows, 16)

    def z_copy(c, s, way):
        t = d + s if way == 0 else d - s
        cc = out_cols(c)
        return remote(
            tok.at[aligned(t * rows, rows, 16), cc], rs.at[slot_of(t, way), cc],
            z_send.at[c, way, s], z_recv.at[c, way, s - 1], right if way == 0 else left,
        )

    def z_in(c, s, way):
        t = d + s if way == 0 else d - s
        part = rs.at[slot_of(t, way), out_cols(c)]
        return remote(part, part, z_send.at[c, way, s], z_recv.at[c, way, s], left if way == 0 else right)

    def partial(target, cc):
        r = aligned(target * rows, rows, 16)
        return jnp.dot(hidden[r, :], wd[:, cc], preferred_element_type=jnp.float32) + jnp.dot(
            wsel[r, :], ret[:, cc], preferred_element_type=jnp.float32
        )

    def hand_on(c, s, way):
        t = d + s if way == 0 else d - s
        r = aligned(t * rows, rows, 16)
        cc = out_cols(c)
        behind = has_left if way == 0 else has_right
        value = partial(t, cc)

        @pl.when(behind)
        def _():
            z_in(c, s, way).wait_recv()
            tok[r, cc] = (value + rs[slot_of(t, way), cc].astype(jnp.float32)).astype(jnp.bfloat16)

        @pl.when(jnp.logical_not(behind))
        def _():
            tok[r, cc] = value.astype(jnp.bfloat16)

        z_copy(c, s, way).start()

    def settle(c):
        cc = out_cols(c)
        value = partial(d, cc)

        @pl.when(has_left & has_right)
        def _():
            z_in(c, 0, 0).wait_recv()
            z_in(c, 0, 1).wait_recv()
            more = rs[slot_of(d, 0), cc].astype(jnp.float32) + rs[slot_of(d, 1), cc].astype(jnp.float32)
            out[:, cc] = (value + more).astype(jnp.bfloat16)

        @pl.when(jnp.logical_not(has_right))
        def _():
            z_in(c, 0, 0).wait_recv()
            out[:, cc] = (value + rs[slot_of(d, 0), cc].astype(jnp.float32)).astype(jnp.bfloat16)

        @pl.when(jnp.logical_not(has_left))
        def _():
            z_in(c, 0, 1).wait_recv()
            out[:, cc] = (value + rs[slot_of(d, 1), cc].astype(jnp.float32)).astype(jnp.bfloat16)

    def valid(c):
        return (c >= 0) & (c < OUT_CHUNKS)

    def z_drain(c):
        for s in range(1, n_dp):
            pl.when(d + s < n_dp)(lambda: z_copy(c, s, 0).wait_send())
            pl.when(d - s >= 0)(lambda: z_copy(c, s, 1).wait_send())

    late = max(OUT_CHUNKS - 3, 0)

    @pl.loop(0, OUT_CHUNKS + n_dp - 1)
    def _(i):
        @pl.when(i < OUT_CHUNKS)
        def _():
            unit = down(i)
            unit.finish()
            unit.complete()
            r_all(i).wait_recv()
            r_own(i).wait()

        c_right, c_left = i - d, i - (n_dp - 1 - d)
        for s in range(n_dp - 1, 0, -1):
            pl.when(valid(c_right) & (d + s < n_dp))(functools.partial(hand_on, c_right, s, 0))
            pl.when(valid(c_left) & (d - s >= 0))(functools.partial(hand_on, c_left, s, 1))

        @pl.when(i + 1 < OUT_CHUNKS)
        def _():
            down(i + 1).spread()

        @pl.when(i + 2 < OUT_CHUNKS)
        def _():
            down(i + 2).begin()
            give_back(i + 2)

        @pl.when((i >= 1) & (i <= OUT_CHUNKS))
        def _():
            down(i - 1).drain()
            r_all(i - 1).wait_send()

        done = i - n_dp - 2
        pl.when((done >= 0) & (done < late))(lambda: z_drain(done))
        c_own = i - jnp.maximum(d, n_dp - 1 - d)
        pl.when(valid(c_own))(functools.partial(settle, c_own))

    for c in range(late, OUT_CHUNKS):
        z_drain(c)


def local(
    tokens, chosen, gate_levels, expert_gate, expert_up, expert_down, shared_gate, shared_up, shared_down,
    *, n_dp, n_e,
):
    rows, width = tokens.shape
    hs = shared_gate.shape[0]
    ffr = expert_gate.shape[2]
    slots = 2 * rows // (n_dp * n_e)
    taken = n_e * n_dp * slots
    pairs = n_e // 2
    links = max(pairs, 5)
    dma = pltpu.SemaphoreType.DMA
    bf16 = jnp.bfloat16
    any_spec = pl.BlockSpec(memory_space=pl.ANY)
    vmem_spec = pl.BlockSpec(memory_space=pltpu.VMEM)
    return pl.pallas_call(
        functools.partial(block_kernel, n_dp, n_e, slots),
        out_shape=jax.ShapeDtypeStruct((rows, width), bf16),
        in_specs=[any_spec] + [vmem_spec] * 2 + [any_spec] * 6,
        out_specs=vmem_spec,
        scratch_shapes=[
            pltpu.VMEM((n_dp * rows, width), bf16),
            pltpu.VMEM((n_e * hs, width), bf16),
            pltpu.VMEM((n_e * hs, width), bf16),
            pltpu.VMEM((n_e * hs, width), bf16),
            pltpu.VMEM((width, ffr), bf16),
            pltpu.VMEM((width, ffr), bf16),
            pltpu.VMEM((2, ffr, width // OUT_CHUNKS), bf16),
            pltpu.VMEM((taken, n_dp * rows), bf16),
            pltpu.VMEM((n_dp * rows, taken), bf16),
            pltpu.VMEM((taken, width), bf16),
            pltpu.VMEM((taken, width), bf16),
            pltpu.VMEM((taken, width), bf16),
            pltpu.VMEM((n_dp * rows, n_e * hs), bf16),
            pltpu.VMEM((taken, ffr), bf16),
            pltpu.VMEM(((n_dp + 1) * rows, width), bf16),
            dma((1,)),
            dma((4,)),
            dma((TOK_CHUNKS, 2, n_dp)),
            dma((TOK_CHUNKS, 2, n_dp)),
            dma((2 * SPLIT,)),
            dma((2 * SPLIT,)),
            dma((2 * SPLIT, links)),
            dma((2 * SPLIT, pairs)),
            dma((OUT_CHUNKS,)),
            dma((OUT_CHUNKS,)),
            dma((OUT_CHUNKS, links)),
            dma((OUT_CHUNKS,)),
            dma((3, TOK_CHUNKS)),
            dma((3, OUT_CHUNKS)),
            dma((OUT_CHUNKS, 2, n_dp)),
            dma((OUT_CHUNKS, 2, n_dp)),
        ],
        compiler_params=pltpu.CompilerParams(
            collective_id=0, has_side_effects=True, vmem_limit_bytes=64 * 2**20 - 2**18
        ),
    )(
        tokens, chosen, gate_levels, shared_gate, shared_up, shared_down,
        expert_gate[0], expert_up[0], expert_down[0],
    )


def solution(mesh):
    both = ("dp", "expert")
    two = P(both, None)
    three = P(both, None, None)
    return jax.shard_map(
        functools.partial(local, n_dp=mesh.shape["dp"], n_e=mesh.shape["expert"]),
        mesh=mesh,
        in_specs=(two, P(), P(), three, three, three, two, two, two),
        out_specs=two,
        check_vma=False,
    )
```

```python
import functools

import jax
import jax.numpy as jnp
from jax import lax
from jax.experimental import pallas as pl
from jax.experimental.pallas import tpu as pltpu
from jax.sharding import PartitionSpec as P

MESH = pl.DeviceIdType.MESH
TOK_CHUNKS = 4
OUT_CHUNKS = 8
SPLIT = 2
NT = (((1,), (1,)), ((), ()))


def flipped(index, mask, bits):
    out = 0
    for b in range(bits):
        bit = (index // (1 << b)) % 2
        if (mask >> b) & 1:
            bit = 1 - bit
        out = out + bit * (1 << b)
    return out


def aligned(index, size, align):
    return pl.ds(pl.multiple_of(index, align), size)


def silu_times(g, v):
    return (g / (1.0 + jnp.exp(-g)) * v).astype(jnp.bfloat16)


def slot_tables(picked, levels, d, e, n_dp, n_e, rows, slots):
    cap = picked.shape[1]
    group = n_dp * slots
    taken = n_e * group

    def spread(a):
        return jnp.concatenate([jnp.broadcast_to(a[j : j + 1], (group, cap)) for j in range(n_e)], axis=0)

    index = spread(picked)
    device = index // rows
    position = (index - device * rows).astype(jnp.float32)
    scale = spread(levels).astype(jnp.float32) / 256.0
    row_of = lax.broadcasted_iota(jnp.int32, (taken, cap), 0)
    slot = (row_of % slots).astype(jnp.float32)
    holder = (row_of // slots) % n_dp
    wanted = jnp.where(device == holder * n_e + e, 1.0, 0.0)
    below = lax.broadcasted_iota(jnp.int32, (cap, cap), 0) <= lax.broadcasted_iota(jnp.int32, (cap, cap), 1)
    rank = jnp.dot(
        wanted.astype(jnp.bfloat16), jnp.where(below, 1.0, 0.0).astype(jnp.bfloat16),
        preferred_element_type=jnp.float32,
    )
    pick = jnp.where(rank == slot + 1.0, wanted, 0.0)
    filled = jnp.sum(pick, axis=1, keepdims=True)
    place = jnp.sum(pick * position, axis=1, keepdims=True)
    weight = jnp.sum(pick * scale, axis=1, keepdims=True)
    of_slot = lax.broadcasted_iota(jnp.int32, (taken, 1), 0)
    start = ((of_slot // slots) % n_dp * rows).astype(jnp.float32)
    column = lax.broadcasted_iota(jnp.int32, (taken, n_dp * rows), 1).astype(jnp.float32)
    hit = jnp.where(column == place + start, 1.0, 0.0)
    return hit * filled, hit * weight


def block_kernel(
    n_dp, n_e, slots,
    tokens, chosen, levels, sh_gate, sh_up, sh_down, ex_gate, ex_up, ex_down,
    out,
    tok, wg, wu, wd, xg, xu, xd, sel, wsel, sbuf, rbuf, ret, hidden, xhid, rs,
    own_sem, stage_sem, tok_send, tok_recv,
    g_loc, g_sent, g_direct, g_sib,
    w_loc, w_sent, w_direct, w_sib,
    a_sem, r_sem, z_send, z_recv,
):
    d = lax.axis_index("dp")
    e = lax.axis_index("expert")
    rows, width = tokens.shape
    hs = sh_gate.shape[0]
    ffr = ex_gate.shape[1]
    tcol = width // TOK_CHUNKS
    col = width // OUT_CHUNKS
    bits = n_e.bit_length() - 1
    pairs = n_e // 2
    relay = pairs == 4
    group = n_dp * slots
    taken = n_e * group

    def dev_e(mask):
        return (d, flipped(e, mask, bits))

    barrier = pltpu.get_barrier_semaphore()
    for j in range(1, n_e):
        pl.semaphore_signal(barrier, inc=1, device_id=dev_e(j), device_id_type=MESH)
    left, right = (d - 1, e), (d + 1, e)
    has_left, has_right = d > 0, d < n_dp - 1
    pl.when(has_left)(lambda: pl.semaphore_signal(barrier, inc=1, device_id=left, device_id_type=MESH))
    pl.when(has_right)(lambda: pl.semaphore_signal(barrier, inc=1, device_id=right, device_id_type=MESH))
    pl.semaphore_wait(barrier, n_e - 1 + jnp.where(has_left, 1, 0) + jnp.where(has_right, 1, 0))

    def remote(src, dst, s, r, dev):
        return pltpu.make_async_remote_copy(
            src_ref=src, dst_ref=dst, send_sem=s, recv_sem=r, device_id=dev, device_id_type=MESH
        )

    near = (1, 2) if relay else tuple(range(1, pairs))

    class Unit:
        def __init__(self, src, buf, r0, rn, cols, sems, u):
            self.src, self.buf, self.r0, self.rn, self.cols = src, buf, r0, rn, cols
            loc, sent, direct, sib = sems
            self.loc, self.sent, self.sib = loc.at[u], sent.at[u], sib.at[u]
            self.got = lambda k: direct.at[u, k]

        def mine(self):
            return self.src.at[pl.ds(self.r0, self.rn), self.cols]

        def spot(self, mask, r0=0, rn=None):
            start = flipped(e, mask, bits) * hs + self.r0 + r0
            return self.buf.at[aligned(start, self.rn if rn is None else rn, 16), self.cols]

        def blocks(self, n):
            return self.buf.at[pl.ds(0, n * self.rn), self.cols]

        def local(self):
            return pltpu.make_async_copy(self.mine(), self.spot(0), self.loc)

        def direct(self, k):
            return remote(self.mine(), self.spot(0), self.sent, self.got(k), dev_e(2 * k))

        def direct_in(self, k):
            part = self.spot(2 * k)
            return remote(part, part, self.sent, self.got(k), dev_e(2 * k))

        def onward(self, i):
            half = self.rn // 2
            part = self.spot(2 * (i + 1), i * half, half)
            return remote(part, part, self.sent, self.got(3 + i), dev_e(2 * (2 - i)))

        def onward_in(self, i):
            half = self.rn // 2
            part = self.spot(6, i * half, half)
            return remote(part, part, self.sent, self.got(3 + i), dev_e(2 * (2 - i)))

        def sibling(self, k):
            src = self.mine() if k == 0 else self.spot(2 * k)
            return remote(src, self.spot(2 * k), self.sent, self.sib, dev_e(1))

        def begin(self):
            for k in near:
                self.direct(k).start()
            self.sibling(0).start()
            self.local().start()

        def arrive(self):
            for k in near:
                self.direct_in(k).wait_recv()
                self.sibling(k).start()

        def pass_on(self):
            if relay:
                for i in range(2):
                    self.onward(i).start()

        def spread(self):
            for k in near:
                self.direct_in(k).wait_recv()
                if relay:
                    self.onward(k - 1).start()
                self.sibling(k).start()

        def finish(self):
            if relay:
                self.onward_in(0).wait_recv()
                self.onward_in(1).wait_recv()
                self.sibling(3).start()

        def complete(self):
            self.local().wait()
            part = self.blocks(pairs)
            remote(part, part, self.sent, self.sib, dev_e(1)).wait_recv()

        def drain(self):
            part = self.blocks(len(near) + (1 if relay else 0) + pairs)
            remote(part, part, self.sent, self.sib, dev_e(1)).wait_send()

    class Lead(Unit):
        def __init__(self, src, buf, r0, rn, cols, sems, u):
            loc, sent, direct, sib = sems
            self.src, self.buf, self.r0, self.rn, self.cols = src, buf, r0, rn, cols
            self.loc, self.sent = loc.at[u], sent.at[u]
            self.sib = sib.at[u, 0]
            self.got = lambda k: direct.at[u, k]
            self.sibs = lambda k: sib.at[u, k]

        def sibling(self, k):
            src = self.mine() if k == 0 else self.spot(2 * k)
            return remote(src, self.spot(2 * k), self.sent, self.sibs(k), dev_e(1))

        def complete(self, ks):
            for k in ks:
                if k == 0:
                    self.local().wait()
                part = self.spot(2 * k + 1)
                remote(part, part, self.sent, self.sibs(k), dev_e(1)).wait_recv()

    g_sems = (g_loc, g_sent, g_direct, g_sib)
    w_sems = (w_loc, w_sent, w_direct, w_sib)
    part_rows = hs // SPLIT
    lead = [
        Lead(src, buf, p * part_rows, part_rows, pl.ds(0, width), g_sems, 2 * p + i)
        for p in range(SPLIT)
        for i, (src, buf) in enumerate(((sh_gate, wg), (sh_up, wu)))
    ]

    def out_cols(c):
        return aligned(c * col, col, col)

    def down(c):
        return Unit(sh_down, wd, 0, hs, out_cols(c), w_sems, c)

    def tok_spot(index, q):
        return tok.at[aligned(index * rows, rows, 16), pl.ds(q * tcol, tcol)]

    def tok_copy(q, h, way):
        index = d - h + 1 if way == 0 else d + h - 1
        src = tokens.at[:, pl.ds(q * tcol, tcol)] if h == 1 else tok_spot(index, q)
        return remote(
            src, tok_spot(index, q), tok_send.at[q, way, h], tok_recv.at[q, way, h], right if way == 0 else left
        )

    def tok_start(q, h):
        pl.when((d - h + 1 >= 0) & has_right)(lambda: tok_copy(q, h, 0).start())
        pl.when((d + h - 1 < n_dp) & has_left)(lambda: tok_copy(q, h, 1).start())

    def tok_wait(q, h):
        @pl.when(d - h >= 0)
        def _():
            part = tok_spot(d - h, q)
            remote(part, part, tok_send.at[q, 0, h], tok_recv.at[q, 0, h], left).wait_recv()

        @pl.when(d + h < n_dp)
        def _():
            part = tok_spot(d + h, q)
            remote(part, part, tok_send.at[q, 1, h], tok_recv.at[q, 1, h], right).wait_recv()

    def tok_drain(q, h):
        pl.when((d - h + 1 >= 0) & has_right)(lambda: tok_copy(q, h, 0).wait_send())
        pl.when((d + h - 1 < n_dp) & has_left)(lambda: tok_copy(q, h, 1).wait_send())

    def group_rows(mask):
        return aligned(flipped(e, mask, bits) * group, group, 16)

    away = pl.ds(0, taken - group)

    def a_out(q, j):
        cc = pl.ds(q * tcol, tcol)
        return remote(sbuf.at[group_rows(j), cc], rbuf.at[group_rows(0), cc], a_sem.at[0, q], a_sem.at[1, q], dev_e(j))

    def a_all(q):
        part = rbuf.at[away, pl.ds(q * tcol, tcol)]
        return remote(part, part, a_sem.at[0, q], a_sem.at[1, q], dev_e(1))

    def a_own(q):
        cc = pl.ds(q * tcol, tcol)
        return pltpu.make_async_copy(sbuf.at[group_rows(0), cc], rbuf.at[group_rows(0), cc], a_sem.at[2, q])

    def r_out(c, j):
        cc = out_cols(c)
        return remote(sbuf.at[group_rows(j), cc], ret.at[group_rows(0), cc], r_sem.at[0, c], r_sem.at[1, c], dev_e(j))

    def r_all(c):
        part = ret.at[away, out_cols(c)]
        return remote(part, part, r_sem.at[0, c], r_sem.at[1, c], dev_e(1))

    def r_own(c):
        cc = out_cols(c)
        return pltpu.make_async_copy(sbuf.at[group_rows(0), cc], ret.at[group_rows(0), cc], r_sem.at[2, c])

    tok_own = pltpu.make_async_copy(tokens, tok.at[aligned(d * rows, rows, 16)], own_sem.at[0])
    tok_start(0, 1)
    for unit in lead[:2]:
        unit.begin()
    tok_start(1, 1)
    tok_own.start()
    for unit in lead[2:]:
        unit.begin()
    stage = [
        pltpu.make_async_copy(src, dst, stage_sem.at[i])
        for i, (src, dst) in enumerate(((ex_gate, xg), (ex_up, xu)))
    ]
    for copy in stage:
        copy.start()

    def fetch(c):
        return pltpu.make_async_copy(ex_down.at[:, out_cols(c)], xd.at[c % 2], stage_sem.at[2 + c % 2])

    fetch(0).start()
    fetch(1).start()

    mine = aligned(d * n_e, n_e, 8)
    one_hot, weighted = slot_tables(chosen[mine, :], levels[mine, :], d, e, n_dp, n_e, rows, slots)
    sel[...] = one_hot.astype(jnp.bfloat16)
    wsel[...] = weighted.T.astype(jnp.bfloat16)
    tok_own.wait()

    def dispatch(q):
        step = min(512, tcol)
        for i in range(tcol // step):
            cc = pl.ds(q * tcol + i * step, step)
            sbuf[:, cc] = jnp.dot(sel[...], tok[:, cc], preferred_element_type=jnp.float32).astype(jnp.bfloat16)
        for j in range(n_e - 1, 0, -1):
            a_out(q, j).start()
        a_own(q).start()

    def early(u):
        lead[u].arrive()
        lead[u].pass_on()

    between = {
        (0, 1): lambda: early(0),
        (0, 2): lambda: early(1),
        (1, 2): lambda: lead[2].arrive(),
        (2, 2): lambda: lead[3].arrive(),
    }
    for q in range(TOK_CHUNKS):
        for h in range(1, n_dp):
            tok_wait(q, h)
            if h < n_dp - 1:
                tok_start(q, h + 1)
            if h == 1 and q + 2 < TOK_CHUNKS:
                tok_start(q + 2, 1)
            if (q, h) in between:
                between[q, h]()
        dispatch(q)
    lead[2].pass_on()
    lead[3].pass_on()
    down(0).begin()
    lead[0].finish()
    lead[1].finish()

    def shared_hidden(start, size):
        r = aligned(start, size, size)
        g = lax.dot_general(tok[...], wg[r, :], NT, preferred_element_type=jnp.float32)
        v = lax.dot_general(tok[...], wu[r, :], NT, preferred_element_type=jnp.float32)
        hidden[:, r] = silu_times(g, v)

    def chip_hidden(k):
        for unit in lead:
            unit.complete((k,))
        shared_hidden(flipped(e, 2 * k, bits) // 2 * (2 * hs), 2 * hs)

    if relay:
        for k in range(3):
            chip_hidden(k)

    for copy in stage:
        copy.wait()
    for q in range(TOK_CHUNKS):
        a_all(q).wait_recv()
        a_own(q).wait()

    @pl.loop(0, ffr // 256)
    def _(i):
        f = aligned(i * 256, 256, 256)
        g = jnp.dot(rbuf[...], xg[:, f], preferred_element_type=jnp.float32)
        v = jnp.dot(rbuf[...], xu[:, f], preferred_element_type=jnp.float32)
        xhid[:, f] = silu_times(g, v)

    for q in range(TOK_CHUNKS):
        a_all(q).wait_send()

    def give_back(c):
        fetch(c).wait()
        sbuf[:, out_cols(c)] = jnp.dot(
            xhid[...], xd[c % 2], preferred_element_type=jnp.float32
        ).astype(jnp.bfloat16)
        pl.when(c + 2 < OUT_CHUNKS)(lambda: fetch(c + 2).start())
        for j in range(n_e - 1, 0, -1):
            r_out(c, j).start()
        r_own(c).start()

    give_back(0)
    lead[2].finish()
    lead[3].finish()
    if relay:
        chip_hidden(3)
    else:
        for unit in lead:
            unit.complete(range(pairs))

        @pl.loop(0, n_e * hs // 256)
        def _(i):
            shared_hidden(i * 256, 256)

    down(0).spread()
    down(1).begin()
    give_back(1)
    for q in range(TOK_CHUNKS):
        for h in range(1, n_dp):
            tok_drain(q, h)
    for unit in lead:
        unit.drain()

    def slot_of(t, way):
        return aligned((t + 1 - way) * rows, rows, 16)

    def z_copy(c, s, way):
        t = d + s if way == 0 else d - s
        cc = out_cols(c)
        return remote(
            tok.at[aligned(t * rows, rows, 16), cc], rs.at[slot_of(t, way), cc],
            z_send.at[c, way, s], z_recv.at[c, way, s - 1], right if way == 0 else left,
        )

    def z_in(c, s, way):
        t = d + s if way == 0 else d - s
        part = rs.at[slot_of(t, way), out_cols(c)]
        return remote(part, part, z_send.at[c, way, s], z_recv.at[c, way, s], left if way == 0 else right)

    def partial(target, cc):
        r = aligned(target * rows, rows, 16)
        return jnp.dot(hidden[r, :], wd[:, cc], preferred_element_type=jnp.float32) + jnp.dot(
            wsel[r, :], ret[:, cc], preferred_element_type=jnp.float32
        )

    def hand_on(c, s, way):
        t = d + s if way == 0 else d - s
        r = aligned(t * rows, rows, 16)
        cc = out_cols(c)
        behind = has_left if way == 0 else has_right
        value = partial(t, cc)

        @pl.when(behind)
        def _():
            z_in(c, s, way).wait_recv()
            tok[r, cc] = (value + rs[slot_of(t, way), cc].astype(jnp.float32)).astype(jnp.bfloat16)

        @pl.when(jnp.logical_not(behind))
        def _():
            tok[r, cc] = value.astype(jnp.bfloat16)

        z_copy(c, s, way).start()

    def settle(c):
        cc = out_cols(c)
        value = partial(d, cc)

        @pl.when(has_left & has_right)
        def _():
            z_in(c, 0, 0).wait_recv()
            z_in(c, 0, 1).wait_recv()
            more = rs[slot_of(d, 0), cc].astype(jnp.float32) + rs[slot_of(d, 1), cc].astype(jnp.float32)
            out[:, cc] = (value + more).astype(jnp.bfloat16)

        @pl.when(jnp.logical_not(has_right))
        def _():
            z_in(c, 0, 0).wait_recv()
            out[:, cc] = (value + rs[slot_of(d, 0), cc].astype(jnp.float32)).astype(jnp.bfloat16)

        @pl.when(jnp.logical_not(has_left))
        def _():
            z_in(c, 0, 1).wait_recv()
            out[:, cc] = (value + rs[slot_of(d, 1), cc].astype(jnp.float32)).astype(jnp.bfloat16)

    def valid(c):
        return (c >= 0) & (c < OUT_CHUNKS)

    def z_drain(c):
        for s in range(1, n_dp):
            pl.when(d + s < n_dp)(lambda: z_copy(c, s, 0).wait_send())
            pl.when(d - s >= 0)(lambda: z_copy(c, s, 1).wait_send())

    late = max(OUT_CHUNKS - 3, 0)

    @pl.loop(0, OUT_CHUNKS + n_dp - 1)
    def _(i):
        @pl.when(i < OUT_CHUNKS)
        def _():
            unit = down(i)
            unit.finish()
            unit.complete()
            r_all(i).wait_recv()
            r_own(i).wait()

        c_right, c_left = i - d, i - (n_dp - 1 - d)
        for s in range(n_dp - 1, 1, -1):
            pl.when(valid(c_right) & (d + s < n_dp))(functools.partial(hand_on, c_right, s, 0))
            pl.when(valid(c_left) & (d - s >= 0))(functools.partial(hand_on, c_left, s, 1))

        def shortest(c, ok, way):
            first = jnp.logical_not(has_left if way == 0 else has_right)
            held = first & (i >= OUT_CHUNKS - 2)
            c = jnp.where(held, c - 1, c)
            pl.when(valid(c) & ok & jnp.logical_not(first & (i == OUT_CHUNKS - 2)))(
                functools.partial(hand_on, c, 1, way)
            )

        shortest(c_right, has_right, 0)
        shortest(c_left, has_left, 1)

        @pl.when(i + 1 < OUT_CHUNKS)
        def _():
            down(i + 1).spread()

        @pl.when(i + 2 < OUT_CHUNKS)
        def _():
            down(i + 2).begin()
            give_back(i + 2)

        @pl.when((i >= 1) & (i <= OUT_CHUNKS))
        def _():
            down(i - 1).drain()
            r_all(i - 1).wait_send()

        done = i - n_dp - 2
        pl.when((done >= 0) & (done < late))(lambda: z_drain(done))
        c_own = i - jnp.maximum(d, n_dp - 1 - d)
        pl.when(valid(c_own))(functools.partial(settle, c_own))

    for c in range(late, OUT_CHUNKS):
        z_drain(c)


def local(
    tokens, chosen, gate_levels, expert_gate, expert_up, expert_down, shared_gate, shared_up, shared_down,
    *, n_dp, n_e,
):
    rows, width = tokens.shape
    hs = shared_gate.shape[0]
    ffr = expert_gate.shape[2]
    slots = 2 * rows // (n_dp * n_e)
    taken = n_e * n_dp * slots
    pairs = n_e // 2
    links = max(pairs, 5)
    dma = pltpu.SemaphoreType.DMA
    bf16 = jnp.bfloat16
    any_spec = pl.BlockSpec(memory_space=pl.ANY)
    vmem_spec = pl.BlockSpec(memory_space=pltpu.VMEM)
    return pl.pallas_call(
        functools.partial(block_kernel, n_dp, n_e, slots),
        out_shape=jax.ShapeDtypeStruct((rows, width), bf16),
        in_specs=[any_spec] + [vmem_spec] * 2 + [any_spec] * 6,
        out_specs=vmem_spec,
        scratch_shapes=[
            pltpu.VMEM((n_dp * rows, width), bf16),
            pltpu.VMEM((n_e * hs, width), bf16),
            pltpu.VMEM((n_e * hs, width), bf16),
            pltpu.VMEM((n_e * hs, width), bf16),
            pltpu.VMEM((width, ffr), bf16),
            pltpu.VMEM((width, ffr), bf16),
            pltpu.VMEM((2, ffr, width // OUT_CHUNKS), bf16),
            pltpu.VMEM((taken, n_dp * rows), bf16),
            pltpu.VMEM((n_dp * rows, taken), bf16),
            pltpu.VMEM((taken, width), bf16),
            pltpu.VMEM((taken, width), bf16),
            pltpu.VMEM((taken, width), bf16),
            pltpu.VMEM((n_dp * rows, n_e * hs), bf16),
            pltpu.VMEM((taken, ffr), bf16),
            pltpu.VMEM(((n_dp + 1) * rows, width), bf16),
            dma((1,)),
            dma((4,)),
            dma((TOK_CHUNKS, 2, n_dp)),
            dma((TOK_CHUNKS, 2, n_dp)),
            dma((2 * SPLIT,)),
            dma((2 * SPLIT,)),
            dma((2 * SPLIT, links)),
            dma((2 * SPLIT, pairs)),
            dma((OUT_CHUNKS,)),
            dma((OUT_CHUNKS,)),
            dma((OUT_CHUNKS, links)),
            dma((OUT_CHUNKS,)),
            dma((3, TOK_CHUNKS)),
            dma((3, OUT_CHUNKS)),
            dma((OUT_CHUNKS, 2, n_dp)),
            dma((OUT_CHUNKS, 2, n_dp)),
        ],
        compiler_params=pltpu.CompilerParams(
            collective_id=0, has_side_effects=True, vmem_limit_bytes=64 * 2**20 - 2**18
        ),
    )(
        tokens, chosen, gate_levels, shared_gate, shared_up, shared_down,
        expert_gate[0], expert_up[0], expert_down[0],
    )


def solution(mesh):
    both = ("dp", "expert")
    two = P(both, None)
    three = P(both, None, None)
    return jax.shard_map(
        functools.partial(local, n_dp=mesh.shape["dp"], n_e=mesh.shape["expert"]),
        mesh=mesh,
        in_specs=(two, P(), P(), three, three, three, two, two, two),
        out_specs=two,
        check_vma=False,
    )
```

```python
import functools

import jax
import jax.numpy as jnp
from jax import lax
from jax.experimental import pallas as pl
from jax.experimental.pallas import tpu as pltpu
from jax.sharding import PartitionSpec as P

MESH = pl.DeviceIdType.MESH
TOK_CHUNKS = 4
OUT_CHUNKS = 8
SPLIT = 2
NT = (((1,), (1,)), ((), ()))


def flipped(index, mask, bits):
    out = 0
    for b in range(bits):
        bit = (index // (1 << b)) % 2
        if (mask >> b) & 1:
            bit = 1 - bit
        out = out + bit * (1 << b)
    return out


def aligned(index, size, align):
    return pl.ds(pl.multiple_of(index, align), size)


def silu_times(g, v):
    return (g / (1.0 + jnp.exp(-g)) * v).astype(jnp.bfloat16)


def slot_tables(picked, levels, d, e, n_dp, n_e, rows, slots):
    cap = picked.shape[1]
    group = n_dp * slots
    taken = n_e * group

    def spread(a):
        return jnp.concatenate([jnp.broadcast_to(a[j : j + 1], (group, cap)) for j in range(n_e)], axis=0)

    index = spread(picked)
    device = index // rows
    position = (index - device * rows).astype(jnp.float32)
    scale = spread(levels).astype(jnp.float32) / 256.0
    row_of = lax.broadcasted_iota(jnp.int32, (taken, cap), 0)
    slot = (row_of % slots).astype(jnp.float32)
    holder = (row_of // slots) % n_dp
    wanted = jnp.where(device == holder * n_e + e, 1.0, 0.0)
    below = lax.broadcasted_iota(jnp.int32, (cap, cap), 0) <= lax.broadcasted_iota(jnp.int32, (cap, cap), 1)
    rank = jnp.dot(
        wanted.astype(jnp.bfloat16), jnp.where(below, 1.0, 0.0).astype(jnp.bfloat16),
        preferred_element_type=jnp.float32,
    )
    pick = jnp.where(rank == slot + 1.0, wanted, 0.0)
    filled = jnp.sum(pick, axis=1, keepdims=True)
    place = jnp.sum(pick * position, axis=1, keepdims=True)
    weight = jnp.sum(pick * scale, axis=1, keepdims=True)
    of_slot = lax.broadcasted_iota(jnp.int32, (taken, 1), 0)
    start = ((of_slot // slots) % n_dp * rows).astype(jnp.float32)
    column = lax.broadcasted_iota(jnp.int32, (taken, n_dp * rows), 1).astype(jnp.float32)
    hit = jnp.where(column == place + start, 1.0, 0.0)
    return hit * filled, hit * weight


def block_kernel(
    n_dp, n_e, slots,
    tokens, chosen, levels, sh_gate, sh_up, sh_down, ex_gate, ex_up, ex_down,
    out,
    tok, wg, wu, wd, xg, xu, xd, sel, wsel, sbuf, rbuf, ret, hidden, xhid, rs,
    own_sem, stage_sem, tok_send, tok_recv,
    g_loc, g_sent, g_direct, g_sib,
    w_loc, w_sent, w_direct, w_sib,
    a_sem, r_sem, z_send, z_recv,
):
    d = lax.axis_index("dp")
    e = lax.axis_index("expert")
    rows, width = tokens.shape
    hs = sh_gate.shape[0]
    ffr = ex_gate.shape[1]
    tcol = width // TOK_CHUNKS
    col = width // OUT_CHUNKS
    bits = n_e.bit_length() - 1
    pairs = n_e // 2
    relay = pairs == 4
    group = n_dp * slots
    taken = n_e * group

    def dev_e(mask):
        return (d, flipped(e, mask, bits))

    barrier = pltpu.get_barrier_semaphore()
    for j in range(1, n_e):
        pl.semaphore_signal(barrier, inc=1, device_id=dev_e(j), device_id_type=MESH)
    left, right = (d - 1, e), (d + 1, e)
    has_left, has_right = d > 0, d < n_dp - 1
    pl.when(has_left)(lambda: pl.semaphore_signal(barrier, inc=1, device_id=left, device_id_type=MESH))
    pl.when(has_right)(lambda: pl.semaphore_signal(barrier, inc=1, device_id=right, device_id_type=MESH))
    pl.semaphore_wait(barrier, n_e - 1 + jnp.where(has_left, 1, 0) + jnp.where(has_right, 1, 0))

    def remote(src, dst, s, r, dev):
        return pltpu.make_async_remote_copy(
            src_ref=src, dst_ref=dst, send_sem=s, recv_sem=r, device_id=dev, device_id_type=MESH
        )

    near = (1, 2) if relay else tuple(range(1, pairs))

    class Unit:
        def __init__(self, src, buf, r0, rn, cols, sems, u):
            self.src, self.buf, self.r0, self.rn, self.cols = src, buf, r0, rn, cols
            loc, sent, direct, sib = sems
            self.loc, self.sent, self.sib = loc.at[u], sent.at[u], sib.at[u]
            self.got = lambda k: direct.at[u, k]

        def mine(self):
            return self.src.at[pl.ds(self.r0, self.rn), self.cols]

        def spot(self, mask, r0=0, rn=None):
            start = flipped(e, mask, bits) * hs + self.r0 + r0
            return self.buf.at[aligned(start, self.rn if rn is None else rn, 16), self.cols]

        def blocks(self, n):
            return self.buf.at[pl.ds(0, n * self.rn), self.cols]

        def local(self):
            return pltpu.make_async_copy(self.mine(), self.spot(0), self.loc)

        def direct(self, k):
            return remote(self.mine(), self.spot(0), self.sent, self.got(k), dev_e(2 * k))

        def direct_in(self, k):
            part = self.spot(2 * k)
            return remote(part, part, self.sent, self.got(k), dev_e(2 * k))

        def onward(self, i):
            half = self.rn // 2
            part = self.spot(2 * (i + 1), i * half, half)
            return remote(part, part, self.sent, self.got(3 + i), dev_e(2 * (2 - i)))

        def onward_in(self, i):
            half = self.rn // 2
            part = self.spot(6, i * half, half)
            return remote(part, part, self.sent, self.got(3 + i), dev_e(2 * (2 - i)))

        def sibling(self, k):
            src = self.mine() if k == 0 else self.spot(2 * k)
            return remote(src, self.spot(2 * k), self.sent, self.sib, dev_e(1))

        def begin(self):
            for k in near:
                self.direct(k).start()
            self.sibling(0).start()
            self.local().start()

        def arrive(self):
            for k in near:
                self.direct_in(k).wait_recv()
                self.sibling(k).start()

        def pass_on(self):
            if relay:
                for i in range(2):
                    self.onward(i).start()

        def spread(self):
            for k in near:
                self.direct_in(k).wait_recv()
                if relay:
                    self.onward(k - 1).start()
                self.sibling(k).start()

        def finish(self):
            if relay:
                self.onward_in(0).wait_recv()
                self.onward_in(1).wait_recv()
                self.sibling(3).start()

        def complete(self):
            self.local().wait()
            part = self.blocks(pairs)
            remote(part, part, self.sent, self.sib, dev_e(1)).wait_recv()

        def drain(self):
            part = self.blocks(len(near) + (1 if relay else 0) + pairs)
            remote(part, part, self.sent, self.sib, dev_e(1)).wait_send()

    class Lead(Unit):
        def __init__(self, src, buf, r0, rn, cols, sems, u):
            loc, sent, direct, sib = sems
            self.src, self.buf, self.r0, self.rn, self.cols = src, buf, r0, rn, cols
            self.loc, self.sent = loc.at[u], sent.at[u]
            self.sib = sib.at[u, 0]
            self.got = lambda k: direct.at[u, k]
            self.sibs = lambda k: sib.at[u, k]

        def sibling(self, k):
            src = self.mine() if k == 0 else self.spot(2 * k)
            return remote(src, self.spot(2 * k), self.sent, self.sibs(k), dev_e(1))

        def complete(self, ks):
            for k in ks:
                if k == 0:
                    self.local().wait()
                part = self.spot(2 * k + 1)
                remote(part, part, self.sent, self.sibs(k), dev_e(1)).wait_recv()

    g_sems = (g_loc, g_sent, g_direct, g_sib)
    w_sems = (w_loc, w_sent, w_direct, w_sib)
    part_rows = hs // SPLIT
    lead = [
        Lead(src, buf, p * part_rows, part_rows, pl.ds(0, width), g_sems, 2 * p + i)
        for p in range(SPLIT)
        for i, (src, buf) in enumerate(((sh_gate, wg), (sh_up, wu)))
    ]

    def out_cols(c):
        return aligned(c * col, col, col)

    def down(c):
        return Unit(sh_down, wd, 0, hs, out_cols(c), w_sems, c)

    def tok_spot(index, q):
        return tok.at[aligned(index * rows, rows, 16), pl.ds(q * tcol, tcol)]

    def tok_copy(q, h, way):
        index = d - h + 1 if way == 0 else d + h - 1
        src = tokens.at[:, pl.ds(q * tcol, tcol)] if h == 1 else tok_spot(index, q)
        return remote(
            src, tok_spot(index, q), tok_send.at[q, way, h], tok_recv.at[q, way, h], right if way == 0 else left
        )

    def tok_start(q, h):
        pl.when((d - h + 1 >= 0) & has_right)(lambda: tok_copy(q, h, 0).start())
        pl.when((d + h - 1 < n_dp) & has_left)(lambda: tok_copy(q, h, 1).start())

    def tok_wait(q, h):
        @pl.when(d - h >= 0)
        def _():
            part = tok_spot(d - h, q)
            remote(part, part, tok_send.at[q, 0, h], tok_recv.at[q, 0, h], left).wait_recv()

        @pl.when(d + h < n_dp)
        def _():
            part = tok_spot(d + h, q)
            remote(part, part, tok_send.at[q, 1, h], tok_recv.at[q, 1, h], right).wait_recv()

    def tok_drain(q, h):
        pl.when((d - h + 1 >= 0) & has_right)(lambda: tok_copy(q, h, 0).wait_send())
        pl.when((d + h - 1 < n_dp) & has_left)(lambda: tok_copy(q, h, 1).wait_send())

    def group_rows(mask):
        return aligned(flipped(e, mask, bits) * group, group, 16)

    away = pl.ds(0, taken - group)

    def a_out(q, j):
        cc = pl.ds(q * tcol, tcol)
        return remote(sbuf.at[group_rows(j), cc], rbuf.at[group_rows(0), cc], a_sem.at[0, q], a_sem.at[1, q], dev_e(j))

    def a_all(q):
        part = rbuf.at[away, pl.ds(q * tcol, tcol)]
        return remote(part, part, a_sem.at[0, q], a_sem.at[1, q], dev_e(1))

    def a_own(q):
        cc = pl.ds(q * tcol, tcol)
        return pltpu.make_async_copy(sbuf.at[group_rows(0), cc], rbuf.at[group_rows(0), cc], a_sem.at[2, q])

    def r_out(c, j):
        cc = out_cols(c)
        return remote(sbuf.at[group_rows(j), cc], ret.at[group_rows(0), cc], r_sem.at[0, c], r_sem.at[1, c], dev_e(j))

    def r_all(c):
        part = ret.at[away, out_cols(c)]
        return remote(part, part, r_sem.at[0, c], r_sem.at[1, c], dev_e(1))

    def r_own(c):
        cc = out_cols(c)
        return pltpu.make_async_copy(sbuf.at[group_rows(0), cc], ret.at[group_rows(0), cc], r_sem.at[2, c])

    tok_own = pltpu.make_async_copy(tokens, tok.at[aligned(d * rows, rows, 16)], own_sem.at[0])
    tok_start(0, 1)
    for unit in lead[:2]:
        unit.begin()
    tok_start(1, 1)
    tok_own.start()
    for unit in lead[2:]:
        unit.begin()
    stage = [
        pltpu.make_async_copy(src, dst, stage_sem.at[i])
        for i, (src, dst) in enumerate(((ex_gate, xg), (ex_up, xu)))
    ]
    for copy in stage:
        copy.start()

    def fetch(c):
        return pltpu.make_async_copy(ex_down.at[:, out_cols(c)], xd.at[c % 2], stage_sem.at[2 + c % 2])

    fetch(0).start()
    fetch(1).start()

    mine = aligned(d * n_e, n_e, 8)
    one_hot, weighted = slot_tables(chosen[mine, :], levels[mine, :], d, e, n_dp, n_e, rows, slots)
    sel[...] = one_hot.astype(jnp.bfloat16)
    wsel[...] = weighted.T.astype(jnp.bfloat16)
    tok_own.wait()

    def dispatch(q):
        step = min(512, tcol)
        for i in range(tcol // step):
            cc = pl.ds(q * tcol + i * step, step)
            sbuf[:, cc] = jnp.dot(sel[...], tok[:, cc], preferred_element_type=jnp.float32).astype(jnp.bfloat16)
        for j in range(n_e - 1, 0, -1):
            a_out(q, j).start()
        a_own(q).start()

    def early(u):
        lead[u].arrive()
        lead[u].pass_on()

    between = {
        (0, 1): lambda: early(0),
        (0, 2): lambda: early(1),
        (1, 2): lambda: lead[2].arrive(),
        (2, 2): lambda: lead[3].arrive(),
    }
    for q in range(TOK_CHUNKS):
        for h in range(1, n_dp):
            tok_wait(q, h)
            if h < n_dp - 1:
                tok_start(q, h + 1)
            if h == 1 and q + 2 < TOK_CHUNKS:
                tok_start(q + 2, 1)
            if (q, h) in between:
                between[q, h]()
        dispatch(q)
    lead[2].pass_on()
    lead[3].pass_on()
    down(0).begin()
    lead[0].finish()
    lead[1].finish()

    def shared_hidden(start, size):
        r = aligned(start, size, size)
        g = lax.dot_general(tok[...], wg[r, :], NT, preferred_element_type=jnp.float32)
        v = lax.dot_general(tok[...], wu[r, :], NT, preferred_element_type=jnp.float32)
        hidden[:, r] = silu_times(g, v)

    def chip_hidden(k):
        for unit in lead:
            unit.complete((k,))
        shared_hidden(flipped(e, 2 * k, bits) // 2 * (2 * hs), 2 * hs)

    if relay:
        for k in range(3):
            chip_hidden(k)

    for copy in stage:
        copy.wait()
    for q in range(TOK_CHUNKS):
        a_all(q).wait_recv()
        a_own(q).wait()

    @pl.loop(0, ffr // 256)
    def _(i):
        f = aligned(i * 256, 256, 256)
        g = jnp.dot(rbuf[...], xg[:, f], preferred_element_type=jnp.float32)
        v = jnp.dot(rbuf[...], xu[:, f], preferred_element_type=jnp.float32)
        xhid[:, f] = silu_times(g, v)

    for q in range(TOK_CHUNKS):
        a_all(q).wait_send()

    def give_back(c):
        fetch(c).wait()
        sbuf[:, out_cols(c)] = jnp.dot(
            xhid[...], xd[c % 2], preferred_element_type=jnp.float32
        ).astype(jnp.bfloat16)
        pl.when(c + 2 < OUT_CHUNKS)(lambda: fetch(c + 2).start())
        for j in range(n_e - 1, 0, -1):
            r_out(c, j).start()
        r_own(c).start()

    give_back(0)
    lead[2].finish()
    lead[3].finish()
    if relay:
        chip_hidden(3)
    else:
        for unit in lead:
            unit.complete(range(pairs))

        @pl.loop(0, n_e * hs // 256)
        def _(i):
            shared_hidden(i * 256, 256)

    down(0).spread()
    down(1).begin()
    give_back(1)
    for q in range(TOK_CHUNKS):
        for h in range(1, n_dp):
            tok_drain(q, h)
    for unit in lead:
        unit.drain()

    def slot_of(t, way):
        return aligned((t + 1 - way) * rows, rows, 16)

    def z_copy(c, s, way):
        t = d + s if way == 0 else d - s
        cc = out_cols(c)
        return remote(
            tok.at[aligned(t * rows, rows, 16), cc], rs.at[slot_of(t, way), cc],
            z_send.at[c, way, s], z_recv.at[c, way, s - 1], right if way == 0 else left,
        )

    def z_in(c, s, way):
        t = d + s if way == 0 else d - s
        part = rs.at[slot_of(t, way), out_cols(c)]
        return remote(part, part, z_send.at[c, way, s], z_recv.at[c, way, s], left if way == 0 else right)

    def partial(target, cc):
        r = aligned(target * rows, rows, 16)
        return jnp.dot(hidden[r, :], wd[:, cc], preferred_element_type=jnp.float32) + jnp.dot(
            wsel[r, :], ret[:, cc], preferred_element_type=jnp.float32
        )

    def hand_on(c, s, way):
        t = d + s if way == 0 else d - s
        r = aligned(t * rows, rows, 16)
        cc = out_cols(c)
        behind = has_left if way == 0 else has_right
        value = partial(t, cc)

        @pl.when(behind)
        def _():
            z_in(c, s, way).wait_recv()
            tok[r, cc] = (value + rs[slot_of(t, way), cc].astype(jnp.float32)).astype(jnp.bfloat16)

        @pl.when(jnp.logical_not(behind))
        def _():
            tok[r, cc] = value.astype(jnp.bfloat16)

        z_copy(c, s, way).start()

    def settle(c):
        cc = out_cols(c)
        value = partial(d, cc)

        @pl.when(has_left & has_right)
        def _():
            z_in(c, 0, 0).wait_recv()
            z_in(c, 0, 1).wait_recv()
            more = rs[slot_of(d, 0), cc].astype(jnp.float32) + rs[slot_of(d, 1), cc].astype(jnp.float32)
            out[:, cc] = (value + more).astype(jnp.bfloat16)

        @pl.when(jnp.logical_not(has_right))
        def _():
            z_in(c, 0, 0).wait_recv()
            out[:, cc] = (value + rs[slot_of(d, 0), cc].astype(jnp.float32)).astype(jnp.bfloat16)

        @pl.when(jnp.logical_not(has_left))
        def _():
            z_in(c, 0, 1).wait_recv()
            out[:, cc] = (value + rs[slot_of(d, 1), cc].astype(jnp.float32)).astype(jnp.bfloat16)

    def valid(c):
        return (c >= 0) & (c < OUT_CHUNKS)

    def z_drain(c):
        for s in range(1, n_dp):
            pl.when(d + s < n_dp)(lambda: z_copy(c, s, 0).wait_send())
            pl.when(d - s >= 0)(lambda: z_copy(c, s, 1).wait_send())

    late = max(OUT_CHUNKS - 3, 0)

    @pl.loop(0, OUT_CHUNKS + n_dp - 1)
    def _(i):
        @pl.when(i < OUT_CHUNKS)
        def _():
            unit = down(i)
            unit.finish()
            unit.complete()
            r_all(i).wait_recv()
            r_own(i).wait()

        c_right, c_left = i - d, i - (n_dp - 1 - d)
        for s in range(n_dp - 1, 1, -1):
            pl.when(valid(c_right) & (d + s < n_dp))(functools.partial(hand_on, c_right, s, 0))
            pl.when(valid(c_left) & (d - s >= 0))(functools.partial(hand_on, c_left, s, 1))

        def shortest(c, ok, way):
            first = jnp.logical_not(has_left if way == 0 else has_right)
            held = first & (i >= OUT_CHUNKS - 2)
            c = jnp.where(held, c - 1, c)
            pl.when(valid(c) & ok & jnp.logical_not(first & (i == OUT_CHUNKS - 2)))(
                functools.partial(hand_on, c, 1, way)
            )

        shortest(c_right, has_right, 0)
        shortest(c_left, has_left, 1)

        @pl.when(i + 1 < OUT_CHUNKS)
        def _():
            down(i + 1).spread()

        @pl.when(i + 2 < OUT_CHUNKS)
        def _():
            down(i + 2).begin()
            give_back(i + 2)

        @pl.when((i >= 1) & (i <= OUT_CHUNKS))
        def _():
            down(i - 1).drain()
            r_all(i - 1).wait_send()

        done = i - n_dp - 2
        pl.when((done >= 0) & (done < late))(lambda: z_drain(done))
        c_own = i - (n_dp - 1)
        pl.when(valid(c_own))(functools.partial(settle, c_own))

    for c in range(late, OUT_CHUNKS):
        z_drain(c)


def local(
    tokens, chosen, gate_levels, expert_gate, expert_up, expert_down, shared_gate, shared_up, shared_down,
    *, n_dp, n_e,
):
    rows, width = tokens.shape
    hs = shared_gate.shape[0]
    ffr = expert_gate.shape[2]
    slots = 2 * rows // (n_dp * n_e)
    taken = n_e * n_dp * slots
    pairs = n_e // 2
    links = max(pairs, 5)
    dma = pltpu.SemaphoreType.DMA
    bf16 = jnp.bfloat16
    any_spec = pl.BlockSpec(memory_space=pl.ANY)
    vmem_spec = pl.BlockSpec(memory_space=pltpu.VMEM)
    return pl.pallas_call(
        functools.partial(block_kernel, n_dp, n_e, slots),
        out_shape=jax.ShapeDtypeStruct((rows, width), bf16),
        in_specs=[any_spec] + [vmem_spec] * 2 + [any_spec] * 6,
        out_specs=vmem_spec,
        scratch_shapes=[
            pltpu.VMEM((n_dp * rows, width), bf16),
            pltpu.VMEM((n_e * hs, width), bf16),
            pltpu.VMEM((n_e * hs, width), bf16),
            pltpu.VMEM((n_e * hs, width), bf16),
            pltpu.VMEM((width, ffr), bf16),
            pltpu.VMEM((width, ffr), bf16),
            pltpu.VMEM((2, ffr, width // OUT_CHUNKS), bf16),
            pltpu.VMEM((taken, n_dp * rows), bf16),
            pltpu.VMEM((n_dp * rows, taken), bf16),
            pltpu.VMEM((taken, width), bf16),
            pltpu.VMEM((taken, width), bf16),
            pltpu.VMEM((taken, width), bf16),
            pltpu.VMEM((n_dp * rows, n_e * hs), bf16),
            pltpu.VMEM((taken, ffr), bf16),
            pltpu.VMEM(((n_dp + 1) * rows, width), bf16),
            dma((1,)),
            dma((4,)),
            dma((TOK_CHUNKS, 2, n_dp)),
            dma((TOK_CHUNKS, 2, n_dp)),
            dma((2 * SPLIT,)),
            dma((2 * SPLIT,)),
            dma((2 * SPLIT, links)),
            dma((2 * SPLIT, pairs)),
            dma((OUT_CHUNKS,)),
            dma((OUT_CHUNKS,)),
            dma((OUT_CHUNKS, links)),
            dma((OUT_CHUNKS,)),
            dma((3, TOK_CHUNKS)),
            dma((3, OUT_CHUNKS)),
            dma((OUT_CHUNKS, 2, n_dp)),
            dma((OUT_CHUNKS, 2, n_dp)),
        ],
        compiler_params=pltpu.CompilerParams(
            collective_id=0, has_side_effects=True, vmem_limit_bytes=64 * 2**20 - 2**18
        ),
    )(
        tokens, chosen, gate_levels, shared_gate, shared_up, shared_down,
        expert_gate[0], expert_up[0], expert_down[0],
    )


def solution(mesh):
    both = ("dp", "expert")
    two = P(both, None)
    three = P(both, None, None)
    return jax.shard_map(
        functools.partial(local, n_dp=mesh.shape["dp"], n_e=mesh.shape["expert"]),
        mesh=mesh,
        in_specs=(two, P(), P(), three, three, three, two, two, two),
        out_specs=two,
        check_vma=False,
    )
```
